32 devices in a mesh: ctx: 4 (over z), tp: 2 (over x), dp: 4 (over y, core).
Axes of the slice: x: 2, y: 2, z: 4, core: 2. Of those that a mesh axis runs over, the one named last changes fastest.
Arguments:
- queries: bfloat16 [4, 1024, 8192], P('dp', 'ctx', 'tp'), may hold values from -80 to 80
- prompt_keys: bfloat16 [4, 1024, 1024], P('dp', 'ctx', 'tp'), may hold values from -4 to 4
- prompt_values: bfloat16 [4, 1024, 1024], P('dp', 'ctx', 'tp'), may hold values from -6 to 6
- resp_keys: bfloat16 [4, 1024, 1024], P('dp', 'ctx', 'tp'), may hold values from -4 to 4
- resp_values: bfloat16 [4, 1024, 1024], P('dp', 'ctx', 'tp'), may hold values from -6 to 6
- pattern: int32 [4, 2, 8], P('dp'), may hold values from 0 to 1, as said below
- lengths: int32 [4, 2], P('dp'), may hold values from 257 to 512, as said below
- out_weight: bfloat16 [8192, 4096], P(('tp', 'dp'), 'ctx'), may hold values from -0.0625 to 0.0625
Outputs:
- attended: bfloat16 [4, 1024, 4096], P('dp', 'ctx', 'tp')
The draws below stay inside these ranges and needn't reach their ends.
Inputs may be any that keep to these rules, and one draw needn't show every extreme that they name: pattern[g, r, 0] is 1 for every response; each response reads 4 or more blocks; in each group some response reads all 8 blocks. `lengths`: in each group some response has length 512.
All inputs are finite; a program needn't handle non-finite values.
Results may differ from the reference program's by a relative error of at most 0.013.
Values may be sent and summed in bfloat16 or wider, within the bound.
A program may use at most 192 MiB of HBM per device.

```python
import jax
import jax.numpy as jnp
from jax import lax

HQ = 64
KVH = 8
HD = 128
WOUT = 4096
BLK = 128
TOK_DEV = 256
RLEN = 512
PROMPT = 1024
RESP = 2
NBLK = 8
GROUPS = 4


def drawn_pair(key):
    key_q = jax.random.fold_in(key, 101)
    key_k = jax.random.fold_in(key, 102)
    shape_q = (GROUPS, RESP * RLEN, HQ * HD)
    shape_k = (GROUPS, PROMPT, KVH * HD)
    keys_drawn = jnp.clip(jax.random.normal(key_k, shape_k, jnp.float32), -4.0, 4.0)
    query_drawn = jnp.clip(jax.random.normal(key_q, shape_q, jnp.float32), -6.0, 6.0)
    return (query_drawn, keys_drawn)


def draw_queries(key, part):
    return drawn_pair(key)[0].astype(jnp.bfloat16)


def draw_prompt_keys(key, part):
    return drawn_pair(key)[1].astype(jnp.bfloat16)


def draw_pattern(key, part):
    key_count = jax.random.fold_in(key, 201)
    key_full = jax.random.fold_in(key, 202)
    key_rank = jax.random.fold_in(key, 203)
    counts = jax.random.randint(key_count, (GROUPS, RESP), 4, NBLK + 1)
    full_resp = jax.random.randint(key_full, (GROUPS,), 0, RESP)
    counts = jnp.where(jnp.arange(RESP, dtype=jnp.int32)[None, :] == full_resp[:, None], NBLK, counts)
    noise = jax.random.randint(key_rank, (GROUPS, RESP, NBLK - 1), 0, 1 << 20)
    noise = noise * NBLK + jnp.arange(NBLK - 1, dtype=jnp.int32)
    order = jnp.argsort(noise, axis=-1, stable=True)
    ranks = jnp.argsort(order, axis=-1, stable=True).astype(jnp.int32)
    rest = (ranks < counts[..., None] - 1).astype(jnp.int32)
    first = jnp.ones((GROUPS, RESP, 1), jnp.int32)
    return jnp.concatenate([first, rest], axis=-1)


def draw_lengths(key, part):
    key_len = jax.random.fold_in(key, 301)
    key_full = jax.random.fold_in(key, 302)
    drawn = jax.random.randint(key_len, (GROUPS, RESP), RLEN // 2 + 1, RLEN + 1)
    full_resp = jax.random.randint(key_full, (GROUPS,), 0, RESP)
    return jnp.where(jnp.arange(RESP, dtype=jnp.int32)[None, :] == full_resp[:, None], RLEN, drawn).astype(jnp.int32)


def block_scale(rng, extent, shards, least, largest):
    def one(axis_at, blocks):
        steps = jax.random.uniform(jax.random.fold_in(jax.random.fold_in(rng, 6), axis_at), (blocks,), jnp.float32, least / len(shards), largest / len(shards))
        return jnp.repeat(jnp.exp(steps), extent[axis_at] // blocks).reshape((-1,) + (1,) * (len(extent) - axis_at - 1))

    gain = one(*shards[0])
    for cut in shards[1:]:
        gain = gain * one(*cut)
    return gain


def bell_draw(rng, extent, scale, bound, cuts=(), kind=jnp.bfloat16):
    values = scale * jax.random.normal(rng, extent, jnp.float32)
    if cuts:
        values = values * block_scale(rng, extent, cuts, -0.22, 0.18)
    return jnp.clip(values, -bound, bound).astype(kind)


def setup_inputs(seed: int = 0) -> dict:
    streams_of = jax.random.split(jax.random.key(seed), 9)
    return {
        "queries": draw_queries(jax.random.fold_in(streams_of[8], 71), 0),
        "prompt_keys": draw_prompt_keys(jax.random.fold_in(streams_of[8], 71), 0),
        "prompt_values": bell_draw(streams_of[2], (GROUPS, PROMPT, KVH * HD), 1.0, 6.0, ((0, 4), (1, 4), (2, 2))),
        "resp_keys": bell_draw(streams_of[3], (GROUPS, RESP * RLEN, KVH * HD), 1.0, 4.0, ((0, 4), (1, 4), (2, 2))),
        "resp_values": bell_draw(streams_of[4], (GROUPS, RESP * RLEN, KVH * HD), 1.0, 6.0, ((0, 4), (1, 4), (2, 2))),
        "pattern": draw_pattern(jax.random.fold_in(streams_of[8], 71), 0),
        "lengths": draw_lengths(jax.random.fold_in(streams_of[8], 71), 0),
        "out_weight": bell_draw(streams_of[7], (HQ * HD, WOUT), (HQ * HD) ** -0.5, 0.0625, ((0, 8), (1, 4))),
    }


def by_response(rows):
    width = rows.shape[-1]
    return jnp.transpose(rows.reshape(2, RESP, TOK_DEV, width), (1, 0, 2, 3)).reshape(RESP, RLEN, width)


def reference(queries, prompt_keys, prompt_values, resp_keys, resp_values, pattern, lengths, out_weight):
    group = HQ // KVH
    scale = HD ** -0.5
    slots = jnp.arange(RLEN, dtype=jnp.int32)
    causal = slots[None, :] <= slots[:, None]

    def one_group(gidx):
        qall = by_response(queries[gidx]).reshape(RESP, RLEN, KVH, group, HD)
        pkeys = prompt_keys[gidx].reshape(PROMPT, KVH, HD)
        pvals = prompt_values[gidx].reshape(PROMPT, KVH, HD)
        rkeys = by_response(resp_keys[gidx]).reshape(RESP, RLEN, KVH, HD)
        rvals = by_response(resp_values[gidx]).reshape(RESP, RLEN, KVH, HD)

        def one_resp(ridx):
            blocks = pattern[gidx, ridx]
            readable = jnp.repeat(blocks, BLK) > 0

            def one_head(kidx):
                qhead = qall[ridx, :, kidx].astype(jnp.float32)
                sprompt = jnp.einsum("igd,jd->gij", qhead, pkeys[:, kidx].astype(jnp.float32)) * scale
                sown = jnp.einsum("igd,jd->gij", qhead, rkeys[ridx, :, kidx].astype(jnp.float32)) * scale
                sprompt = jnp.where(readable[None, None, :], sprompt, -jnp.inf)
                sown = jnp.where(causal[None], sown, -jnp.inf)
                top = jnp.maximum(jnp.max(sprompt, -1), jnp.max(sown, -1))
                eprompt = jnp.where(readable[None, None, :], jnp.exp(sprompt - top[..., None]), 0.0)
                eown = jnp.where(causal[None], jnp.exp(sown - top[..., None]), 0.0)
                total = jnp.sum(eprompt, -1) + jnp.sum(eown, -1)
                rprompt = eprompt.astype(jnp.bfloat16).astype(jnp.float32)
                rown = eown.astype(jnp.bfloat16).astype(jnp.float32)
                mixed = jnp.einsum("gij,jd->gid", rprompt, pvals[:, kidx].astype(jnp.float32), precision=lax.Precision.HIGHEST)
                mixed = mixed + jnp.einsum("gij,jd->gid", rown, rvals[ridx, :, kidx].astype(jnp.float32), precision=lax.Precision.HIGHEST)
                return mixed / total[..., None]

            heads = lax.map(one_head, jnp.arange(KVH, dtype=jnp.int32))
            context = jnp.transpose(heads, (2, 0, 1, 3)).reshape(RLEN, HQ * HD)
            live = slots < lengths[gidx, ridx]
            return jnp.where(live[:, None], context, 0.0).astype(jnp.bfloat16)

        context = lax.map(one_resp, jnp.arange(RESP, dtype=jnp.int32)).reshape(RESP * RLEN, HQ * HD)
        projected = jnp.dot(context, out_weight, preferred_element_type=jnp.float32).astype(jnp.bfloat16)
        projected = jnp.transpose(projected.reshape(RESP, 2, TOK_DEV, WOUT), (1, 0, 2, 3))
        return projected.reshape(RESP * RLEN, WOUT)

    return lax.map(one_group, jnp.arange(GROUPS, dtype=jnp.int32))
```

```python
import jax
import jax.numpy as jnp
from jax import lax
from jax.experimental import pallas as pl
from jax.experimental.pallas import tpu as pltpu
from jax.sharding import PartitionSpec as P

HD = 128
BLK = 128
RLEN = 512


def shifted(x, axis, by):
    devices = lax.axis_size(axis)
    pairs = [(i, i + by) for i in range(devices) if 0 <= i + by < devices]
    return lax.ppermute(x, axis, pairs)


def local(
    queries, prompt_keys, prompt_values, resp_keys, resp_values, pattern, lengths, out_weight
):
    tok = queries.shape[1]
    kv_here = prompt_keys.shape[2] // HD
    q_here = queries.shape[2] // HD
    group = q_here // kv_here
    scale = HD ** (-0.5)
    halves = RLEN // tok
    responses = lax.axis_size("ctx") // halves
    place = lax.axis_index("ctx")
    resp_id = place % responses
    half = place // responses
    positions = half * tok + jnp.arange(tok, dtype=jnp.int32)
    chosen = jnp.arange(pattern.shape[1], dtype=jnp.int32) == resp_id
    block_row = jnp.sum(jnp.where(chosen[:, None], pattern[0], 0), axis=0)
    live_len = jnp.sum(jnp.where(chosen, lengths[0], 0))
    query_heads = queries[0].reshape(tok, kv_here, group, HD)
    earlier = shifted((resp_keys, resp_values), "ctx", responses)
    own_keys = jnp.concatenate([earlier[0][0], resp_keys[0]], axis=0).reshape(2 * tok, kv_here, HD)
    own_vals = jnp.concatenate([earlier[1][0], resp_values[0]], axis=0).reshape(
        2 * tok, kv_here, HD
    )
    key_pos = (half - 1) * tok + jnp.arange(2 * tok, dtype=jnp.int32)
    allowed = (key_pos[None, :] >= 0) & (key_pos[None, :] <= positions[:, None])
    scores = (
        jnp.einsum("ikgd,jkd->kgij", query_heads, own_keys, preferred_element_type=jnp.float32)
        * scale
    )
    running = jnp.max(jnp.where(allowed, scores, -jnp.inf), axis=-1)
    probs = jnp.where(allowed, jnp.exp(scores - running[..., None]), 0.0)
    total = jnp.sum(probs, axis=-1)
    accum = jnp.einsum(
        "kgij,jkd->kgid", probs.astype(jnp.bfloat16), own_vals, preferred_element_type=jnp.float32
    )
    pieces = (
        lax.all_gather(prompt_keys, "ctx", axis=1, tiled=True),
        lax.all_gather(prompt_values, "ctx", axis=1, tiled=True),
    )
    count = pieces[0].shape[1]
    block_ids = jnp.arange(count, dtype=jnp.int32) // BLK
    onehot = block_ids[:, None] == jnp.arange(block_row.shape[0], dtype=jnp.int32)[None, :]
    readable = jnp.sum(jnp.where(onehot, block_row[None, :], 0), axis=1) > 0
    piece_keys = pieces[0][0].reshape(-1, kv_here, HD)
    piece_vals = pieces[1][0].reshape(-1, kv_here, HD)
    block_scores = (
        jnp.einsum("ikgd,jkd->kgij", query_heads, piece_keys, preferred_element_type=jnp.float32)
        * scale
    )
    mask = readable[None, None, None, :]
    new_max = jnp.maximum(running, jnp.max(jnp.where(mask, block_scores, -jnp.inf), axis=-1))
    weights = jnp.where(mask, jnp.exp(block_scores - new_max[..., None]), 0.0)
    factor = jnp.exp(running - new_max)
    new_total = total * factor + jnp.sum(weights, axis=-1)
    new_acc = accum * factor[..., None] + jnp.einsum(
        "kgij,jkd->kgid",
        weights.astype(jnp.bfloat16),
        piece_vals,
        preferred_element_type=jnp.float32,
    )
    context = new_acc / new_total[..., None]
    context = jnp.transpose(context, (2, 0, 1, 3)).reshape(tok, q_here * HD)
    context = jnp.where((positions < live_len)[:, None], context, 0.0).astype(jnp.bfloat16)
    head_rows = lax.all_gather(out_weight, "dp", axis=0, tiled=True)
    partial_out = jnp.dot(
        context,
        lax.all_gather(head_rows, "ctx", axis=1, tiled=True),
        preferred_element_type=jnp.float32,
    )
    summed = lax.psum_scatter(
        partial_out.astype(jnp.bfloat16), "tp", scatter_dimension=1, tiled=True
    )
    return summed[None]


MESH = pl.DeviceIdType.MESH
CHUNKS = 4


def kernel(
    q_ref, pk_ref, pv_ref, rk_ref, rv_ref, bias_ref, live_ref, w_ref, o_ref,
    kbuf, vbuf, ctx, wbuf, part, rbuf,
    kv_send, kv_recv, rs_send, rs_recv, own_sem,
    w_recv, w_send, fz_send, fy_send, c_send, c_recv, p_send, p_recv,
):
    z = lax.axis_index("ctx")
    t = lax.axis_index("tp")
    d = lax.axis_index("dp")
    y, k = d // 2, d % 2
    kz = z % 2
    tok = q_ref.shape[0]
    rows = w_ref.shape[0] // CHUNKS
    wide = w_ref.shape[1]
    pair_out = z // 2

    def dev(zz, tt, yy, kk):
        return {"ctx": zz, "tp": tt, "dp": yy * 2 + kk}

    barrier = pltpu.get_barrier_semaphore()
    greeted = [dev((z + i) % 4, t, y, k) for i in (1, 2, 3)]
    greeted += [dev((z + i) % 4, t, y, 1 - k) for i in range(4)]
    greeted += [dev(z, t, 1 - y, kk) for kk in range(2)]
    greeted += [dev(z, 1 - t, y, kk) for kk in range(2)]
    for other in greeted:
        pl.semaphore_signal(barrier, inc=1, device_id=other, device_id_type=MESH)
    pl.semaphore_wait(barrier, len(greeted))

    def remote(src, dst, send, recv, where):
        return pltpu.make_async_remote_copy(
            src_ref=src, dst_ref=dst, send_sem=send, recv_sem=recv,
            device_id=where, device_id_type=MESH,
        )

    def arrived(ref, sem):
        pltpu.make_async_copy(ref, ref, sem).wait()

    def prompt_rows(buf, zz):
        return buf.at[pl.ds(pl.multiple_of(zz * tok, tok), tok), :]

    pre = 4 * tok
    kv = ((pk_ref, kbuf), (pv_ref, vbuf))
    rkv = ((rk_ref, kbuf), (rv_ref, vbuf))
    kv_copies = []
    for step in (1, 3, 2):
        for i, (src, buf) in enumerate(kv):
            kv_copies.append(
                remote(src, prompt_rows(buf, z), kv_send.at[i, step], kv_recv.at[i, step],
                       dev((z + step) % 4, t, y, k))
            )
    for i, (src, buf) in enumerate(rkv):
        kv_copies.append(
            remote(src, buf.at[pl.ds(pre, tok), :], rs_send.at[i], rs_recv.at[i],
                   dev((z + 2) % 4, t, y, k))
        )
    for copy in kv_copies:
        copy.start()
    own = []
    for i, (src, buf) in enumerate(kv):
        own.append(pltpu.make_async_copy(src, prompt_rows(buf, z), own_sem.at[i]))
    for i, (src, buf) in enumerate(rkv):
        own.append(
            pltpu.make_async_copy(src, buf.at[pl.ds(pre + tok, tok), :], own_sem.at[2 + i])
        )
    for copy in own:
        copy.start()

    def w_slot(cc, dd, j):
        return wbuf.at[cc, dd, pl.ds(pl.multiple_of(j * rows, rows), rows), :]

    def own_rows(j):
        return w_ref.at[pl.ds(pl.multiple_of(j * rows, rows), rows), :]

    def own_send(target, j, where):
        return remote(own_rows(j), w_slot(pair_out, d, j), w_send.at[target, j],
                      w_recv.at[pair_out, d, j], where)

    targets = (
        (z < 3, dev(jnp.minimum(z + 1, 3), t, y, kz)),
        (z > 0, dev(jnp.maximum(z - 1, 0), t, y, kz)),
        (z >= 0, dev(z, t, 1 - y, kz)),
        (k != kz, dev(z, t, y, 1 - k)),
    )

    def each_own(act):
        @pl.loop(0, CHUNKS)
        def _(j):
            for n, (cond, where) in enumerate(targets):
                @pl.when(cond)
                def _(n=n, where=where):
                    act(own_send(n, j, where))

    each_own(lambda copy: copy.start())

    @pl.when(k == kz)
    def _():
        @pl.loop(0, CHUNKS)
        def _(j):
            pltpu.make_async_copy(
                own_rows(j), w_slot(pair_out, d, j), w_recv.at[pair_out, d, j]
            ).start()

    two = k != kz
    middle = (z == 1) | (z == 2)
    near_hi = z >= 2
    cc_a = jnp.where(two, jnp.where(near_hi, 1, 0), 1 - pair_out)
    cc_b = 1 - cc_a

    def forwards(cc, n):
        c = k + 2 * cc
        dd = y * 2 + n // CHUNKS
        j = n % CHUNKS
        ref, rec = w_slot(cc, dd, j), w_recv.at[cc, dd, j]
        up = (c < z) & (z < 3)
        down = (c > z) & (z > 0)
        zz = jnp.where(up, jnp.minimum(z + 1, 3), jnp.maximum(z - 1, 0))
        along = remote(ref, ref, fz_send.at[cc, n], rec, dev(zz, t, y, k))
        across = remote(ref, ref, fy_send.at[cc, n], rec, dev(z, t, 1 - y, k))
        return ref, rec, up | down, along, across

    def relay(cc, n):
        ref, rec, onward, along, across = forwards(cc, n)
        arrived(ref, rec)

        @pl.when(onward)
        def _():
            along.start()

        across.start()

    for copy in own:
        copy.wait()
    for step in (1, 3, 2):
        for i, (_, buf) in enumerate(kv):
            arrived(prompt_rows(buf, (z + 4 - step) % 4), kv_recv.at[i, step])
    for i, (_, buf) in enumerate(rkv):
        arrived(buf.at[pl.ds(pre, tok), :], rs_recv.at[i])

    scale = HD ** (-0.5)
    heads = q_ref.shape[1] // HD
    kv_here = rk_ref.shape[1] // HD
    group = heads // kv_here
    per = 2
    mine = pl.ds(pl.multiple_of(k * tok, tok), tok)

    def head(kk, g):
        col = pl.multiple_of((kk * group + g) * HD, HD)
        kcol = pl.multiple_of(kk * HD, HD)
        gcol = pl.multiple_of(g * HD, HD)
        s = lax.dot_general(
            q_ref[:, pl.ds(col, HD)], kbuf[:, pl.ds(kcol, HD)], (((1,), (1,)), ((), ())),
            preferred_element_type=jnp.float32,
        )
        s = s * scale + bias_ref[...]
        p = jnp.exp(s - jnp.max(s, axis=-1, keepdims=True))
        total = jnp.sum(p, axis=-1, keepdims=True)
        o = jnp.dot(p.astype(jnp.bfloat16), vbuf[:, pl.ds(kcol, HD)],
                    preferred_element_type=jnp.float32)
        o = jnp.where(live_ref[...] > 0, o / total, 0.0)
        ctx[kk, mine, pl.ds(gcol, HD)] = o.astype(jnp.bfloat16)

    def ctx_send(kk):
        ref = ctx.at[kk, mine, :]
        return remote(ref, ref, c_send.at[kk], c_recv.at[kk], dev(z, t, y, 1 - k))

    steps = heads // per
    per_kv = group // per
    slots = 2 * CHUNKS

    @pl.loop(0, steps)
    def _(it):
        kk = it // per_kv
        for u in range(per):
            head(kk, (it % per_kv) * per + u)

        @pl.when(it % per_kv == per_kv - 1)
        def _():
            ctx_send(kk).start()

        @pl.when(two & (it < slots))
        def _():
            relay(cc_a, it)

            @pl.when(middle)
            def _():
                relay(cc_b, it)

        @pl.when(jnp.logical_not(two) & (it >= steps - slots))
        def _():
            relay(cc_a, it - (steps - slots))

    theirs = pl.ds(pl.multiple_of((1 - k) * tok, tok), tok)

    @pl.loop(0, kv_here)
    def _(kk):
        arrived(ctx.at[kk, theirs, :], c_recv.at[kk])

    tile = 256

    def out_send(cc, kk):
        return remote(
            part.at[cc, pl.ds(kk * tok, tok), :], rbuf.at[t, k], p_send.at[cc, kk],
            p_recv.at[t, k], dev(z, cc, y, kk),
        )

    def out_sends(cc, act):
        for kk in range(2):
            @pl.when((cc != t) | (k != kk))
            def _():
                act(out_send(cc, kk))

    def project(cc):
        @pl.loop(0, slots)
        def _(n):
            dd = (1 - y) * 2 + n // CHUNKS
            arrived(w_slot(cc, dd, n % CHUNKS), w_recv.at[cc, dd, n % CHUNKS])

        @pl.when(k + 2 * cc == z)
        def _():
            @pl.loop(0, slots)
            def _(n):
                dd = y * 2 + n // CHUNKS
                arrived(w_slot(cc, dd, n % CHUNKS), w_recv.at[cc, dd, n % CHUNKS])

        @pl.loop(0, wide // tile)
        def _(n):
            cols = pl.ds(pl.multiple_of(n * tile, tile), tile)
            acc = jnp.dot(ctx[0], wbuf[cc, 0, :, cols], preferred_element_type=jnp.float32)
            for dd in range(1, kv_here):
                acc += jnp.dot(
                    ctx[dd], wbuf[cc, dd, :, cols], preferred_element_type=jnp.float32
                )
            part[cc, :, cols] = acc.astype(jnp.bfloat16)

        @pl.when(cc == t)
        def _():
            rbuf[t, k] = part[cc, mine, :]

        out_sends(cc, lambda copy: copy.start())

    first = jnp.where(two, cc_a, cc_b)
    second = 1 - first
    project(first)

    @pl.when(two & jnp.logical_not(middle))
    def _():
        @pl.loop(0, slots)
        def _(n):
            relay(cc_b, n)

    project(second)

    for copy in kv_copies:
        copy.wait_send()
    each_own(lambda copy: copy.wait_send())

    def drain(cc):
        @pl.loop(0, slots)
        def _(n):
            _, _, onward, along, across = forwards(cc, n)

            @pl.when(onward)
            def _():
                along.wait_send()

            across.wait_send()

    drain(cc_a)

    @pl.when(two)
    def _():
        drain(cc_b)

    @pl.loop(0, kv_here)
    def _(kk):
        ctx_send(kk).wait_send()

    for src in range(2):
        for half in range(2):
            @pl.when((t != src) | (k != half))
            def _(src=src, half=half):
                arrived(rbuf.at[src, half], p_recv.at[src, half])
    for half in range(2):
        both = rbuf[0, half].astype(jnp.float32) + rbuf[1, half].astype(jnp.float32)
        o_ref[:, half * wide:(half + 1) * wide] = both.astype(jnp.bfloat16)
    for cc in range(2):
        out_sends(cc, lambda copy: copy.wait_send())


def fused(
    queries, prompt_keys, prompt_values, resp_keys, resp_values, pattern, lengths, out_weight
):
    tok = queries.shape[1]
    halves = RLEN // tok
    responses = lax.axis_size("ctx") // halves
    place = lax.axis_index("ctx")
    resp_id = place % responses
    half = place // responses
    chosen = jnp.arange(pattern.shape[1], dtype=jnp.int32) == resp_id
    block_row = jnp.sum(jnp.where(chosen[:, None], pattern[0], 0), axis=0)
    live_len = jnp.sum(jnp.where(chosen, lengths[0], 0))
    slot = jnp.arange(tok, dtype=jnp.int32)
    readable = jnp.repeat(block_row, BLK) > 0
    earlier = jnp.broadcast_to(half > 0, (tok,))
    keys_ok = jnp.concatenate([readable, earlier, jnp.ones((tok,), jnp.bool_)])
    later = jnp.arange(keys_ok.shape[0], dtype=jnp.int32) - (keys_ok.shape[0] - tok)
    allowed = keys_ok[None, :] & (later[None, :] <= slot[:, None])
    bias = jnp.where(allowed, 0.0, -jnp.inf).astype(jnp.float32)
    live = jnp.broadcast_to((half * tok + slot < live_len)[:, None], (tok, HD)).astype(jnp.float32)
    span = keys_ok.shape[0]
    kvw = prompt_keys.shape[2]
    kv_here = kvw // HD
    wr, wide = out_weight.shape
    bf = jnp.bfloat16
    dma = pltpu.SemaphoreType.DMA
    vm = pl.BlockSpec(memory_space=pltpu.VMEM)
    anywhere = pl.BlockSpec(memory_space=pl.ANY)
    slots = 2 * CHUNKS
    out = pl.pallas_call(
        kernel,
        out_shape=jax.ShapeDtypeStruct((tok, 2 * wide), bf),
        in_specs=[vm, anywhere, anywhere, anywhere, anywhere, vm, vm, anywhere],
        out_specs=vm,
        scratch_shapes=[
            pltpu.VMEM((span, kvw), bf),
            pltpu.VMEM((span, kvw), bf),
            pltpu.VMEM((kv_here, 2 * tok, wr), bf),
            pltpu.VMEM((2, kv_here, wr, wide), bf),
            pltpu.VMEM((2, 2 * tok, wide), bf),
            pltpu.VMEM((2, 2, tok, wide), bf),
            dma((2, 4)), dma((2, 4)), dma((2,)), dma((2,)), dma((4,)),
            dma((2, kv_here, CHUNKS)), dma((4, CHUNKS)), dma((2, slots)), dma((2, slots)),
            dma((kv_here,)), dma((kv_here,)), dma((2, 2)), dma((2, 2)),
        ],
        compiler_params=pltpu.CompilerParams(
            collective_id=0, has_side_effects=True, vmem_limit_bytes=60 << 20
        ),
    )(
        queries[0], prompt_keys[0], prompt_values[0], resp_keys[0], resp_values[0],
        bias, live, out_weight,
    )
    return out[None]


def solution(mesh):
    placed = (
        P("dp", "ctx", "tp"),
        P("dp", "ctx", "tp"),
        P("dp", "ctx", "tp"),
        P("dp", "ctx", "tp"),
        P("dp", "ctx", "tp"),
        P("dp", None, None),
        P("dp", None),
        P(("tp", "dp"), "ctx"),
    )
    sizes = (mesh.shape["ctx"], mesh.shape["tp"], mesh.shape["dp"])
    body = fused if sizes == (4, 2, 4) else local
    return jax.shard_map(
        body, mesh=mesh, in_specs=placed, out_specs=P("dp", "ctx", "tp"), check_vma=False
    )
```
